32 devices in a mesh: ctx: 4 (over y, x), tp: 8 (over z, core).
Axes of the slice: x: 2, y: 2, z: 4, core: 2. Of those that a mesh axis runs over, the one named last changes fastest.
Arguments:
- tokens: bfloat16 [3072, 8192], P('ctx', 'tp'), may hold values from -6 to 6
- w_in: bfloat16 [8192, 3, 4096], P(None, None, 'tp'), may hold values from -0.0625 to 0.0625
- short_taps: bfloat16 [3, 3, 4096], P(None, None, 'tp'), may hold values from -3 to 3
- long_taps: bfloat16 [128, 4096], P(None, 'tp'), may hold values from -0.5 to 0.5
- skip_gain: float32 [4096], P('tp'), may hold values from 0.5 to 1.5
- w_out: bfloat16 [4096, 8192], P('tp'), may hold values from -0.125 to 0.125
Outputs:
- mixed: bfloat16 [3072, 8192], P('ctx', 'tp')
The draws below stay inside these ranges and needn't reach their ends.
All inputs are finite; a program needn't handle non-finite values.
Results may differ from the reference program's by a relative error of at most 0.014.
Values may be sent and summed in bfloat16 or wider, within the bound.
No kernel may reach another device: no remote copies, remote signals or barrier semaphores. Data moves between devices by JAX's collectives and lax.ppermute only.
A program may use at most 256 MiB of HBM per device.

```python
import jax
import jax.numpy as jnp
from jax import lax

D = 8192
C = 4096
FILT = 128
SHORT = 3
TOKENS = 3072
N_TP = 8


def spiked(drawn, rng, source, target, parts, factor):
    owner, partner = [(jnp.arange(drawn.shape[position]) // (drawn.shape[position] // parts)).reshape([-1 if axis == position else 1 for axis in range(drawn.ndim)]) for position in (source, target)]
    chosen = jax.random.permutation(rng, parts)[partner]
    strong = (owner == chosen) | (owner == (partner + parts // 2) % parts)
    return jnp.where(strong, factor * drawn, drawn)


def block_levels(rng, shape, shards, low, top_value):
    factor_of = 1.0
    for position, blocks in shards:
        draws = jax.random.uniform(jax.random.fold_in(jax.random.fold_in(rng, 6), position), (blocks,), jnp.float32, low / len(shards), top_value / len(shards))
        factor_of = factor_of * jnp.repeat(jnp.exp(draws), shape[position] // blocks).reshape((-1,) + (1,) * (len(shape) - 1 - position))
    return factor_of


def normal_values(own_key, shape, deviation, reach, pieces=(), kind=jnp.bfloat16):
    factor_of = block_levels(own_key, shape, pieces, -0.22, 0.18) if pieces else 1.0
    result = jax.random.normal(own_key, shape, jnp.float32) * deviation * factor_of
    return jnp.minimum(jnp.maximum(result, -reach), reach).astype(kind)


def noise_with(rng, shape, scale, limit, shards, heavy, kind=jnp.bfloat16):
    result = scale * jax.random.normal(rng, shape, jnp.float32)
    if shards:
        result = result * block_levels(rng, shape, shards, -0.22, 0.18)
    return jnp.clip(spiked(result, jax.random.fold_in(rng, 3), *heavy), -limit, limit).astype(kind)


def setup_inputs(seed: int = 0) -> dict:
    key_of = jax.random.split(jax.random.key(seed), 7)
    tokens = normal_values(key_of[0], (TOKENS, D), 1.0, 6.0, ((0, 4), (1, 8)))
    w_in = normal_values(key_of[1], (D, 3, C), D ** -0.5, 0.0625, ((2, 8),))
    short_taps = normal_values(key_of[2], (3, SHORT, C), 0.6, 3.0, ((2, 8),))
    long_taps = normal_values(key_of[3], (FILT, C), 0.09, 0.5, ((1, 8),))
    skip_gain = jnp.clip(0.5 + 1.0 * jax.random.uniform(key_of[4], (C,), jnp.float32) ** block_levels(key_of[4], (C,), ((0, 8),), -0.2, 0.2), 0.5, 1.5)
    w_out = noise_with(key_of[5], (C, D), C ** -0.5, 0.125, ((0, 8),), (0, 1, 8, 2.0))
    return dict(tokens=tokens, w_in=w_in, short_taps=short_taps, long_taps=long_taps, skip_gain=skip_gain, w_out=w_out)


def reference(tokens, w_in, short_taps, long_taps, skip_gain, w_out):
    proj = jnp.dot(tokens, w_in.reshape(D, 3 * C), preferred_element_type=jnp.float32)
    u_low = proj.astype(jnp.bfloat16)
    u_full = lax.optimization_barrier(u_low).astype(jnp.float32).reshape(TOKENS, 3, C)
    taps = short_taps.astype(jnp.float32)
    mixed_short = jnp.zeros((TOKENS, 3, C), jnp.float32)
    for k in range(SHORT):
        moved = jnp.pad(u_full, ((k, 0), (0, 0), (0, 0)))[:TOKENS]
        mixed_short = mixed_short + taps[:, k, :][None] * moved
    z_low = (mixed_short[:, 1] * mixed_short[:, 2]).astype(jnp.bfloat16)
    z_full = lax.optimization_barrier(z_low).astype(jnp.float32)
    padded = jnp.pad(z_full, ((FILT, 0), (0, 0)))
    long_full = long_taps.astype(jnp.float32)

    def tap_step(total, k):
        moved = lax.dynamic_slice_in_dim(padded, (FILT - k).astype(jnp.int32), TOKENS, 0)
        row = lax.dynamic_slice_in_dim(long_full, k.astype(jnp.int32), 1, 0)
        return total + row * moved, None

    filtered, _ = lax.scan(tap_step, jnp.zeros((TOKENS, C), jnp.float32), jnp.arange(FILT, dtype=jnp.int32))
    filtered = filtered + skip_gain[None] * z_full
    gated = (mixed_short[:, 0] * filtered).astype(jnp.bfloat16)
    group = C // N_TP
    gated_groups = gated.reshape(TOKENS, N_TP, group).transpose(1, 0, 2)
    weight_groups = w_out.reshape(N_TP, group, D)

    def group_step(total, pair):
        part = jnp.dot(pair[0], pair[1], preferred_element_type=jnp.float32).astype(jnp.bfloat16)
        return total + lax.optimization_barrier(part).astype(jnp.float32), None

    summed, _ = lax.scan(group_step, jnp.zeros((TOKENS, D), jnp.float32), (gated_groups, weight_groups))
    return summed.astype(jnp.bfloat16)
```

```python
import jax
import jax.numpy as jnp
from jax import lax
from jax.experimental import pallas as pl
from jax.experimental.pallas import tpu as pltpu
from jax.sharding import PartitionSpec as P

FILT = 128
SHORT = 3
HALO = 144
LANES = 128
F32 = jnp.float32
BF16 = jnp.bfloat16


def from_behind(value, axis, steps):
    count = lax.axis_size(axis)
    first, last = (max(0, -steps), min(count, count - steps))
    return lax.ppermute(value, axis, [(source, source + steps) for source in range(first, last)])


def mix_kernel(u0, u1, u2, short_ref, long_ref, skip_ref, g_ref, wide, shifted, taps_f):
    rows = g_ref.shape[0]
    span = rows + FILT
    tile = next(size for size in (64, 48, 32, 16) if rows % size == 0)
    taps_f[...] = long_ref[...].astype(F32)
    short = short_ref[...].astype(F32)

    def stream(j, ref, begin, count):
        total = None
        for k in range(SHORT):
            term = short[j, k : k + 1, :] * wide[j, pl.ds(begin - k, count), :]
            total = term if total is None else total + term
        return total

    for j, ref in enumerate((u0, u1, u2)):
        wide[j] = ref[...].astype(F32)
    lead = HALO - FILT
    z = (stream(1, u1, lead, span) * stream(2, u2, lead, span)).astype(BF16).astype(F32)
    shifted[0, pl.ds(0, 8), :] = jnp.zeros((8, LANES), F32)
    shifted[0, pl.ds(8, span), :] = z
    for r in range(1, 8):
        shifted[r, pl.ds(8, span), :] = shifted[0, pl.ds(8 - r, span), :]

    def one_tile(i, carry):
        begin = pl.multiple_of(i * tile, 16)
        total = jnp.zeros((tile, LANES), F32)
        for r in range(8):
            window = shifted[r, pl.ds(begin + 16, tile + FILT - 8), :]
            for q in range(FILT // 8):
                at = FILT - 8 - 8 * q
                k = 8 * q + r
                total = total + taps_f[k : k + 1, :] * window[at : at + tile]
        total = total + skip_ref[...] * shifted[0, pl.ds(begin + FILT + 8, tile), :]
        gate = None
        for k in range(SHORT):
            term = short[0, k : k + 1, :] * wide[0, pl.ds(begin + HALO - k, tile), :]
            gate = term if gate is None else gate + term
        g_ref[pl.ds(begin, tile), :] = (gate * total).astype(BF16)
        return carry

    lax.fori_loop(0, rows // tile, one_tile, 0)


def mix(extended, short_taps, long_taps, skip_gain):
    local = long_taps.shape[1]
    blocks = local // LANES
    rows = extended.shape[0] - HALO
    stream_spec = lambda j: pl.BlockSpec((HALO + rows, LANES), lambda i: (0, j * blocks + i))
    return pl.pallas_call(
        mix_kernel,
        out_shape=jax.ShapeDtypeStruct((rows, local), BF16),
        grid=(blocks,),
        in_specs=[
            stream_spec(0),
            stream_spec(1),
            stream_spec(2),
            pl.BlockSpec((3, SHORT, LANES), lambda i: (0, 0, i)),
            pl.BlockSpec((FILT, LANES), lambda i: (0, i)),
            pl.BlockSpec((1, LANES), lambda i: (0, i)),
        ],
        out_specs=pl.BlockSpec((rows, LANES), lambda i: (0, i)),
        scratch_shapes=[
            pltpu.VMEM((3, HALO + rows, LANES), F32),
            pltpu.VMEM((8, 8 + FILT + rows, LANES), F32),
            pltpu.VMEM((FILT, LANES), F32),
        ],
        cost_estimate=pl.CostEstimate(
            flops=300 * rows * local, bytes_accessed=8 * rows * local, transcendentals=0
        ),
        name="mix",
    )(extended, extended, extended, short_taps, long_taps, skip_gain[None])


def body(tokens, w_in, short_taps, long_taps, skip_gain, w_out):
    rows = tokens.shape[0]
    streams = jnp.transpose(w_in, (1, 0, 2))
    gathered = lax.all_gather(tokens, "tp", axis=1, tiled=True)
    u = jnp.concatenate(
        [
            jnp.dot(gathered, streams[j], preferred_element_type=F32).astype(BF16)
            for j in range(3)
        ],
        axis=1,
    )
    edge = from_behind(u[rows - HALO :], "ctx", 1)
    gated = mix(jnp.concatenate([edge, u], axis=0), short_taps, long_taps, skip_gain)
    terms = jnp.dot(gated, w_out, preferred_element_type=F32).astype(BF16)
    return lax.psum_scatter(terms, "tp", scatter_dimension=1, tiled=True)


def solution(mesh):
    in_specs = (
        P("ctx", "tp"),
        P(None, None, "tp"),
        P(None, None, "tp"),
        P(None, "tp"),
        P("tp"),
        P("tp", None),
    )
    out_specs = P("ctx", "tp")
    return jax.shard_map(body, mesh=mesh, in_specs=in_specs, out_specs=out_specs, check_vma=False)
```

```python
import functools

import jax
import jax.numpy as jnp
from jax import lax
from jax.experimental import pallas as pl
from jax.experimental.pallas import tpu as pltpu
from jax.sharding import PartitionSpec as P


FILT = 128
SHORT = 3
HALO = 144
LANES = 128
F32 = jnp.float32
BF16 = jnp.bfloat16


def from_behind(value, axis, steps):
    count = lax.axis_size(axis)
    first, last = (max(0, -steps), min(count, count - steps))
    return lax.ppermute(value, axis, [(source, source + steps) for source in range(first, last)])


def mix_kernel(u0, u1, u2, short_ref, long_ref, skip_ref, g_ref, wide, shifted, taps_f):
    rows = g_ref.shape[0]
    span = rows + FILT
    tile = next(size for size in (112, 96, 80, 64, 48, 32, 16) if rows % size == 0)
    taps_f[...] = long_ref[...].astype(F32)
    short = short_ref[...].astype(F32)

    def stream(j, begin, count):
        total = None
        for k in range(SHORT):
            term = short[j, k : k + 1, :] * wide[j, pl.ds(begin - k, count), :]
            total = term if total is None else total + term
        return total

    for j, ref in enumerate((u0, u1, u2)):
        wide[j] = ref[...].astype(F32)
    lead = HALO - FILT
    z = (stream(1, lead, span) * stream(2, lead, span)).astype(BF16).astype(F32)
    shifted[0, pl.ds(0, 8), :] = jnp.zeros((8, LANES), F32)
    shifted[0, pl.ds(8, span), :] = z
    for r in range(1, 8):
        shifted[r, pl.ds(8, span), :] = shifted[0, pl.ds(8 - r, span), :]

    def one_tile(i, carry):
        begin = pl.multiple_of(i * tile, 16)
        total = jnp.zeros((tile, LANES), F32)
        for r in range(8):
            window = shifted[r, pl.ds(begin + 16, tile + FILT - 8), :]
            for q in range(FILT // 8):
                at = FILT - 8 - 8 * q
                k = 8 * q + r
                total = total + taps_f[k : k + 1, :] * window[at : at + tile]
        total = total + skip_ref[...] * shifted[0, pl.ds(begin + FILT + 8, tile), :]
        gate = None
        for k in range(SHORT):
            term = short[0, k : k + 1, :] * wide[0, pl.ds(begin + HALO - k, tile), :]
            gate = term if gate is None else gate + term
        g_ref[pl.ds(begin, tile), :] = (gate * total).astype(BF16)
        return carry

    lax.fori_loop(0, rows // tile, one_tile, 0)


def mix(extended, short_taps, long_taps, skip_gain):
    local = long_taps.shape[1]
    blocks = local // LANES
    rows = extended.shape[0] - HALO
    stream_spec = lambda j: pl.BlockSpec((HALO + rows, LANES), lambda i: (0, j * blocks + i))
    return pl.pallas_call(
        mix_kernel,
        out_shape=jax.ShapeDtypeStruct((rows, local), BF16),
        grid=(blocks,),
        in_specs=[
            stream_spec(0),
            stream_spec(1),
            stream_spec(2),
            pl.BlockSpec((3, SHORT, LANES), lambda i: (0, 0, i)),
            pl.BlockSpec((FILT, LANES), lambda i: (0, i)),
            pl.BlockSpec((1, LANES), lambda i: (0, i)),
        ],
        out_specs=pl.BlockSpec((rows, LANES), lambda i: (0, i)),
        scratch_shapes=[
            pltpu.VMEM((3, HALO + rows, LANES), F32),
            pltpu.VMEM((8, 8 + FILT + rows, LANES), F32),
            pltpu.VMEM((FILT, LANES), F32),
        ],
        compiler_params=pltpu.CompilerParams(vmem_limit_bytes=14 << 20),
        cost_estimate=pl.CostEstimate(
            flops=300 * rows * local, bytes_accessed=8 * rows * local, transcendentals=0
        ),
        name="mix",
    )(extended, extended, extended, short_taps, long_taps, skip_gain[None])


def project_kernel(carries, order, w_hbm, *refs):
    if carries:
        carried, refs = refs[0], refs[1:]
    sources, u_ref, held, weight, total, sems, w_sems = (
        refs[:-6], refs[-6], refs[-5], refs[-4], refs[-3], refs[-2], refs[-1]
    )
    count = len(sources)
    rows, depth = held.shape[1:]
    local = weight.shape[3]
    tile = next(size for size in (480, 288, 240, 192, 144, 128, 96, 80, 48, 16) if rows % size == 0)
    pairs = []
    for k, source in enumerate(sources):
        at = pl.ds(pl.multiple_of(order[k] * depth, depth), depth)
        pairs.append(
            (
                pltpu.make_async_copy(source, held.at[k], sems.at[k]),
                pltpu.make_async_copy(w_hbm.at[:, at, :], weight.at[k], w_sems.at[k]),
            )
        )
    for pair in pairs[:2]:
        for copy in pair:
            copy.start()
    for k, pair in enumerate(pairs):
        for copy in pair:
            copy.wait()
        for copy in pairs[k + 2] if k + 2 < count else ():
            copy.start()
        starts = k == 0
        ends = k == count - 1

        def one_tile(i, carry):
            at = pl.ds(pl.multiple_of(i * tile, 16), tile)
            for j in range(3):
                span = pl.ds(j * local, local)
                part = jnp.dot(held[k, at, :], weight[k, j], preferred_element_type=F32)
                if not starts:
                    part = total[at, span] + part
                elif carries:
                    part = carried[at, span] + part
                if ends:
                    u_ref[at, span] = part.astype(u_ref.dtype)
                else:
                    total[at, span] = part
            return carry

        lax.fori_loop(0, rows // tile, one_tile, 0)


def project(blocks, order, streams, carried, kind):
    rows, depth = blocks[0].shape
    local = streams.shape[2]
    count = len(blocks)
    extra = [] if carried is None else [carried]
    return pl.pallas_call(
        functools.partial(project_kernel, bool(extra)),
        out_shape=jax.ShapeDtypeStruct((rows, 3 * local), kind),
        in_specs=[pl.BlockSpec(memory_space=pltpu.SMEM)]
        + [pl.BlockSpec(memory_space=pl.ANY)]
        + [pl.BlockSpec(memory_space=pltpu.VMEM)] * len(extra)
        + [pl.BlockSpec(memory_space=pl.ANY)] * count,
        out_specs=pl.BlockSpec(memory_space=pltpu.VMEM),
        scratch_shapes=[
            pltpu.VMEM((count, rows, depth), BF16),
            pltpu.VMEM((count, 3, depth, local), BF16),
            pltpu.VMEM((rows, 3 * local), F32),
            pltpu.SemaphoreType.DMA((count,)),
            pltpu.SemaphoreType.DMA((count,)),
        ],
        compiler_params=pltpu.CompilerParams(vmem_limit_bytes=58 << 20),
        cost_estimate=pl.CostEstimate(
            flops=6 * rows * local * depth * count,
            bytes_accessed=2 * depth * count * rows,
            transcendentals=0,
        ),
        name="project",
    )(order, streams, *extra, *blocks)


NEAR = ((0, 1), (1, 0), (2, 3), (3, 2))
INNER = ((1, 2), (2, 1))
OUTWARD = ((1, 0), (2, 3))
INWARD = ((0, 1), (3, 2))


def along(value, hops):
    return lax.ppermute(
        value, "tp", [(2 * a + core, 2 * b + core) for a, b in hops for core in (0, 1)]
    )


def partner(value):
    return lax.ppermute(value, "tp", [(d, d ^ 1) for d in range(lax.axis_size("tp"))])


def after(value, *others):
    return lax.optimization_barrier((value, *others))[0]


def line_body(tokens, w_in, short_taps, long_taps, skip_gain, w_out):
    rows, width = tokens.shape
    streams = jnp.transpose(w_in, (1, 0, 2))
    me = lax.axis_index("tp")
    chip, core = me // 2, me % 2
    inner = (chip == 1) | (chip == 2)
    slots = lax.iota(jnp.int32, 4)
    early = 2 * (chip ^ (slots // 2)) + (core ^ (slots % 2))
    flip = jnp.where(inner, 3, 2)
    late = 2 * (chip ^ flip ^ (slots // 2)) + (core ^ (slots % 2))

    def columns(b, owner):
        return lax.dynamic_slice_in_dim(w_out, (2 * (chip ^ b) + owner) * width, width, 1)

    own = [columns(b, core) for b in range(4)]
    lent = [columns(b, 1 - core) for b in range(4)]
    borrowed = [partner(piece) for piece in lent]
    weights = [jnp.concatenate(pair, axis=0) for pair in zip(own, borrowed)]

    def shared(pieces):
        return [part for piece in pieces for part in (piece, partner(piece))]

    def spread(x):
        near = along(x, NEAR)
        middle = along(x, INNER)
        outer = along(middle, OUTWARD)
        second = along(near, INNER)
        final = along(second, OUTWARD)
        return x, near, (middle, outer), jnp.where(inner, second, final)

    order = jnp.concatenate([early, late])

    def gather(parts, previous):
        if previous is not None:
            middle, outer = parts[2]
            parts = (*parts[:2], jnp.where(inner, middle, after(outer, *previous)), parts[3])
        else:
            parts = (*parts[:2], jnp.where(inner, *parts[2]), parts[3])
        blocks = shared(parts[:2]) + shared(parts[2:])
        if previous is not None:
            blocks[0] = after(blocks[0], *previous)
        partial = project(blocks[:6], order[:6], streams, None, F32)
        return project(blocks[6:], order[6:], streams, partial, BF16), partial

    def filtered(extended):
        return mix(extended, short_taps, long_taps, skip_gain)

    def spend(gated):
        both = jnp.concatenate([gated, partner(gated)], axis=1)

        def term(b):
            return jnp.dot(both, weights[b], preferred_element_type=F32).astype(BF16)

        far, cross = term(3), term(2)
        first = along(far, INWARD)
        second = along(cross, INWARD)
        return far, cross, term(1), term(0), first, second

    def scatter(terms, gates):
        far, cross, near, mine, first, second = terms
        if gates:
            first, second = after(first, gates[0]), after(second, gates[1])
        first = along(cross + first, INNER)
        second = along(far + second, INNER)
        if gates:
            first = after(first, gates[1])
        last = along(near + first, NEAR)
        total = mine.astype(F32) + second.astype(F32) + last.astype(F32)
        return total.astype(BF16)

    upper = rows * 3 // 8 // 16 * 16
    parts = [spread(tokens[upper:]), spread(tokens[:upper])]
    u_last, _ = gather(parts[0], None)
    edge = from_behind(u_last[rows - upper - HALO :], "ctx", 1)
    terms_a = spend(filtered(u_last))
    u_first, partial = gather(parts[1], terms_a[:2])
    half = upper * 2 // 3 // 16 * 16
    gated = [
        filtered(jnp.concatenate([edge, u_first[:half]], axis=0)),
        filtered(jnp.concatenate([u_first[half - HALO :], u_last[:HALO]], axis=0)),
    ]
    terms_b = spend(jnp.concatenate(gated, axis=0))
    out_a = scatter(terms_a, (partial, gated[0]))
    out_b = scatter(terms_b, None)
    return jnp.concatenate([out_b, out_a], axis=0)


def plain_body(tokens, w_in, short_taps, long_taps, skip_gain, w_out):
    rows = tokens.shape[0]
    streams = jnp.transpose(w_in, (1, 0, 2))
    gathered = lax.all_gather(tokens, "tp", axis=1, tiled=True)
    u = jnp.concatenate(
        [
            jnp.dot(gathered, streams[j], preferred_element_type=F32).astype(BF16)
            for j in range(3)
        ],
        axis=1,
    )
    edge = from_behind(u[rows - HALO :], "ctx", 1)
    gated = mix(jnp.concatenate([edge, u], axis=0), short_taps, long_taps, skip_gain)
    terms = jnp.dot(gated, w_out, preferred_element_type=F32).astype(BF16)
    return lax.psum_scatter(terms, "tp", scatter_dimension=1, tiled=True)


def solution(mesh):
    in_specs = (
        P("ctx", "tp"),
        P(None, None, "tp"),
        P(None, None, "tp"),
        P(None, "tp"),
        P("tp"),
        P("tp", None),
    )
    out_specs = P("ctx", "tp")
    specs = dict(mesh=mesh, in_specs=in_specs, out_specs=out_specs, check_vma=False)
    if mesh.shape["tp"] != 8:
        return jax.shard_map(plain_body, **specs)

    return jax.shard_map(line_body, **specs)
```
